32 devices in a mesh: row: 4 (over y, x), col: 8 (over z, core).
Axes of the slice: x: 2, y: 2, z: 4, core: 2. Of those that a mesh axis runs over, the one named last changes fastest.
Arguments:
- tokens: bfloat16 [128, 8192], P('col', 'row'), may hold values from -6 to 6
- out_grad: bfloat16 [128, 8192], P('col', 'row'), may hold values from -6 to 6
- gate_weight: bfloat16 [8192, 29568], P('row', 'col'), may hold values from -0.0625 to 0.0625
- up_weight: bfloat16 [8192, 29568], P('row', 'col'), may hold values from -0.0625 to 0.0625
- down_weight: bfloat16 [29568, 8192], P('col', 'row'), may hold values from -0.03125 to 0.03125
Outputs:
- input_grad: bfloat16 [128, 8192], P('col', 'row')
- gate_wgrad: bfloat16 [8192, 29568], P('row', 'col')
- up_wgrad: bfloat16 [8192, 29568], P('row', 'col')
- down_wgrad: bfloat16 [29568, 8192], P('col', 'row')
The draws below stay inside these ranges and needn't reach their ends.
All inputs are finite; a program needn't handle non-finite values.
Results may differ from the reference program's by a relative error of at most 0.005.
Values may be sent and summed in bfloat16 or wider, within the bound.
A program may use at most 192 MiB of HBM per device.

```python
import math
import jax
import jax.numpy as jnp
from jax import lax

D = 8192
FF = 29568
TOKENS = 128


def block_scale(stream_key, shape, shards, least, top_value):
    loudness = 1.0
    for axis_at, parts in shards:
        heights = jax.random.uniform(jax.random.fold_in(jax.random.fold_in(stream_key, 6), axis_at), (parts,), jnp.float32, least / len(shards), top_value / len(shards))
        loudness = loudness * jnp.repeat(jnp.exp(heights), shape[axis_at] // parts).reshape((-1,) + (1,) * (len(shape) - 1 - axis_at))
    return loudness


def bell_draw(own_key, dims, width, reach, shards=(), kind=jnp.bfloat16):
    values = width * jax.random.normal(own_key, dims, jnp.float32)
    if shards:
        values = values * block_scale(own_key, dims, shards, -0.22, 0.18)
    return jnp.clip(values, -reach, reach).astype(kind)


def setup_inputs(seed: int = 0) -> dict:
    splits = jax.random.split(jax.random.key(seed), 6)
    return {
        "tokens": bell_draw(splits[0], (TOKENS, D), 1.0, 6.0, ((0, 8), (1, 4))),
        "out_grad": bell_draw(splits[1], (TOKENS, D), 1.0, 6.0, ((0, 8), (1, 4))),
        "gate_weight": bell_draw(splits[2], (D, FF), D ** -0.5, 0.0625, ((0, 4), (1, 8))),
        "up_weight": bell_draw(splits[3], (D, FF), D ** -0.5, 0.0625, ((0, 4), (1, 8))),
        "down_weight": bell_draw(splits[4], (FF, D), FF ** -0.5, 0.03125, ((0, 8), (1, 4))),
    }


def contract(left, right, left_dim, right_dim):
    return lax.dot_general(left, right, (((left_dim,), (right_dim,)), ((), ())), preferred_element_type=jnp.float32)

def reference(tokens, out_grad, gate_weight, up_weight, down_weight):
    factor = 1.0 / math.sqrt(TOKENS)
    gate = jnp.dot(tokens, gate_weight, preferred_element_type=jnp.float32)
    upward = jnp.dot(tokens, up_weight, preferred_element_type=jnp.float32)
    hid_grad = contract(out_grad, down_weight, 1, 1)
    sig = jax.nn.sigmoid(gate)
    act = gate * sig
    hidden = (act * upward).astype(jnp.bfloat16)
    gate_grad = (hid_grad * upward * sig * (1.0 + gate * (1.0 - sig))).astype(jnp.bfloat16)
    up_grad = (hid_grad * act).astype(jnp.bfloat16)
    input_grad = (contract(gate_grad, gate_weight, 1, 1) + contract(up_grad, up_weight, 1, 1)).astype(jnp.bfloat16)
    gate_wgrad = (contract(tokens, gate_grad, 0, 0) * factor).astype(jnp.bfloat16)
    up_wgrad = (contract(tokens, up_grad, 0, 0) * factor).astype(jnp.bfloat16)
    down_wgrad = (contract(hidden, out_grad, 0, 0) * factor).astype(jnp.bfloat16)
    return (input_grad, gate_wgrad, up_wgrad, down_wgrad)
```

```python
import functools
import math

import jax
import jax.numpy as jnp
from jax import lax
from jax.experimental import pallas as pl
from jax.experimental.pallas import tpu as pltpu
from jax.sharding import PartitionSpec as P

STEP = 512
BF16 = jnp.bfloat16
F32 = jnp.float32


def flip(index, bits):
    low = lax.rem(lax.rem(index, 2) + bits % 2, 2)
    high = lax.rem(lax.div(index, 2) + bits // 2, 2)
    return high * 2 + low


def dots(left, right, left_dim, right_dim):
    return lax.dot_general(
        left, right, (((left_dim,), (right_dim,)), ((), ())), preferred_element_type=F32
    )


def forward_kernel(
    n_col, hidden_units,
    tok_ref, og_ref, gw_hbm, uw_hbm, dw_hbm,
    pan, res, pieces,
    gw, uw, dw, own, sbuf, rbuf, acc,
    w_sem, ag_send, ag_recv, fw_send, fw_recv, rs_send, rs_recv, out_send, out_recv,
):
    row = lax.axis_index("row")
    col = lax.axis_index("col")
    tb = tok_ref.shape[0]
    tokens = pan.shape[1]
    part = tokens // 4
    n_chip = n_col // 2
    per = part // tb
    full = hidden_units // STEP
    tail = hidden_units - full * STEP
    tail_pad = own.shape[2] - full * STEP

    loads = [
        pltpu.make_async_copy(src, dst, w_sem.at[i])
        for i, (src, dst) in enumerate(((gw_hbm, gw), (uw_hbm, uw), (dw_hbm, dw)))
    ]
    for load in loads:
        load.start()

    partner = lax.rem(col, 2) * -2 + 1 + col
    barrier = pltpu.get_barrier_semaphore()
    for s in range(1, 4):
        pl.semaphore_signal(barrier, inc=1, device_id={"row": flip(row, s), "col": col})
    for j in range(1, n_chip):
        pl.semaphore_signal(
            barrier, inc=1, device_id={"row": row, "col": lax.rem(col + 2 * j, n_col)}
        )
    pl.semaphore_signal(barrier, inc=1, device_id={"row": row, "col": partner})

    def slot(c):
        block = lax.div(c, per)
        low = lax.rem(lax.rem(block, 2) + lax.rem(row, 2), 2)
        high = lax.rem(lax.div(block, 2) + lax.div(row, 2), 2)
        at = (high * 2 + low) * part + lax.rem(c, per) * tb
        return pl.ds(pl.multiple_of(at, tb), tb)

    inputs = (tok_ref, og_ref)
    if tail:
        for a in range(3):
            own[a, :, full * STEP :] = jnp.zeros((part, tail_pad), F32)
            sbuf[a, :, full * STEP :] = jnp.zeros((3 * part, tail_pad), BF16)

    pl.semaphore_wait(barrier, 3 + n_chip)

    def remote(src, dst, send, recv, c, r=row):
        return pltpu.make_async_remote_copy(
            src_ref=src, dst_ref=dst, send_sem=send, recv_sem=recv,
            device_id={"row": r, "col": c}, device_id_type=pl.DeviceIdType.MESH,
        )

    def gather(a, j):
        to = partner if j == 0 else lax.rem(col + 2 * j, n_col)
        return remote(inputs[a], pan.at[a, slot(col)], ag_send.at[a, j], ag_recv.at[a, j], to)

    def forward(a, j):
        at = slot(lax.rem(col + 2 * (n_chip - j), n_col))
        return remote(pan.at[a, at], pan.at[a, at], fw_send.at[a, j], fw_recv.at[a, j], partner)

    for a in range(2):
        for j in range(n_chip):
            gather(a, (j + 1) % n_chip).start()
    for a in range(2):
        pan[a, slot(col), :] = inputs[a][...]
    for a in range(2):
        for j in range(1, n_chip):
            gather(a, j).wait_recv()
            forward(a, j).start()

    def gathered(a):
        gather(a, 0).wait_recv()
        for j in range(1, n_chip):
            forward(a, j).wait_recv()

    def span(at, size):
        if isinstance(at, int):
            return pl.ds(at, size)
        return pl.ds(pl.multiple_of(at, 128), size)

    def scatter(a, s, g, at, width):
        cols = span(at, width)
        return remote(
            sbuf.at[a, pl.ds((s - 1) * part, part), cols],
            rbuf.at[a, s - 1, :, cols],
            rs_send.at[a, s - 1, g], rs_recv.at[a, s - 1, g], col, flip(row, s),
        )

    def spread(s, g, at, width):
        cols = span(at, width)
        return remote(
            res.at[:, pl.ds(0, part), cols],
            res.at[:, pl.ds(s * part, part), cols],
            out_send.at[s - 1, g], out_recv.at[s - 1, g], col, flip(row, s),
        )

    def each_group(body):
        @pl.loop(0, full)
        def _(g):
            body(g, g * STEP, STEP, STEP)

        if tail:
            body(full, full * STEP, tail, tail_pad)

    def first(a, g, at, width, padded):
        cols = span(at, width)
        if a == 2:
            value = dots(pan[1], dw[cols, :], 1, 1)
        else:
            value = dots(pan[0], (gw, uw)[a][:, cols], 1, 0)
        own[a, :, cols] = value[:part]
        sbuf[a, :, cols] = value[part:].astype(BF16)
        for s in range(1, 4):
            scatter(a, s, g, at, padded).start()

    gathered(0)
    loads[0].wait()
    each_group(functools.partial(first, 0))
    loads[1].wait()
    each_group(functools.partial(first, 1))
    gathered(1)
    loads[2].wait()
    each_group(functools.partial(first, 2))

    def middle(g, at, width, padded):
        cols = span(at, padded)
        sums = []
        for a in range(3):
            for s in range(1, 4):
                scatter(a, s, g, at, padded).wait_recv()
            terms = [rbuf[a, s, :, cols].astype(F32) for s in range(3)]
            sums.append((own[a, :, cols] + terms[0]) + (terms[1] + terms[2]))
        gate, upward, hid_grad = sums
        sig = jax.nn.sigmoid(gate)
        act = gate * sig
        res[0, 0:part, cols] = (act * upward).astype(BF16)
        res[1, 0:part, cols] = (
            hid_grad * upward * sig * (1.0 + gate * (1.0 - sig))
        ).astype(BF16)
        res[2, 0:part, cols] = (hid_grad * act).astype(BF16)
        for s in range(1, 4):
            spread(s, g, at, padded).start()

    each_group(middle)
    acc[...] = jnp.zeros_like(acc)

    def last(g, at, width, padded):
        cols = span(at, width)
        for s in range(1, 4):
            spread(s, g, at, padded).wait_recv()
        acc[...] += dots(res[1, :, cols], gw[:, cols], 1, 1) + dots(
            res[2, :, cols], uw[:, cols], 1, 1
        )

    each_group(last)
    for s in range(n_col):
        pieces[s] = acc[slot(lax.rem(col + s, n_col)), :].astype(BF16)

    def drain(g, at, width, padded):
        for s in range(1, 4):
            spread(s, g, at, padded).wait_send()
            for a in range(3):
                scatter(a, s, g, at, padded).wait_send()

    each_group(drain)
    for a in range(2):
        for j in range(n_chip):
            gather(a, j).wait_send()
            if j:
                forward(a, j).wait_send()


def weight_kernel(
    hidden_units, factor, tok, og, hid, gg, ug, gate_out, up_out, down_out
):
    full = hidden_units // STEP
    turned = jnp.transpose(tok[0].astype(F32)).astype(BF16)

    def write(at, width):
        cols = pl.ds(at, width) if isinstance(at, int) else pl.ds(pl.multiple_of(at, 128), width)
        gate_out[:, cols] = (dots(turned, gg[0, :, cols], 1, 0) * factor).astype(BF16)
        up_out[:, cols] = (dots(turned, ug[0, :, cols], 1, 0) * factor).astype(BF16)

    @pl.loop(0, full)
    def _(g):
        write(g * STEP, STEP)

    if hidden_units % STEP:
        write(full * STEP, hidden_units % STEP)
    hid_turned = jnp.transpose(hid[0].astype(F32)).astype(BF16)

    @pl.loop(0, og.shape[2] // STEP)
    def _(g):
        cols = pl.ds(pl.multiple_of(g * STEP, 128), STEP)
        down_out[:, cols] = (dots(hid_turned, og[0, :, cols], 1, 0) * factor).astype(BF16)


def local(n_col, tokens, out_grad, gate_weight, up_weight, down_weight):
    tb, width = tokens.shape
    total = tb * n_col
    part = total // 4
    units = gate_weight.shape[1]
    padded = -(-units // 128) * 128
    groups = -(-units // STEP)
    n_chip = n_col // 2
    vmem = pl.BlockSpec(memory_space=pltpu.VMEM)
    hbm = pl.BlockSpec(memory_space=pl.ANY)
    dma = pltpu.SemaphoreType.DMA
    pan, res, pieces = pl.pallas_call(
        functools.partial(forward_kernel, n_col, units),
        out_shape=(
            jax.ShapeDtypeStruct((2, total, width), BF16),
            jax.ShapeDtypeStruct((3, total, padded), BF16),
            jax.ShapeDtypeStruct((n_col, tb, width), BF16),
        ),
        in_specs=[vmem, vmem, hbm, hbm, hbm],
        out_specs=(vmem, vmem, vmem),
        scratch_shapes=[
            pltpu.VMEM(gate_weight.shape, BF16),
            pltpu.VMEM(up_weight.shape, BF16),
            pltpu.VMEM(down_weight.shape, BF16),
            pltpu.VMEM((3, part, padded), F32),
            pltpu.VMEM((3, 3 * part, padded), BF16),
            pltpu.VMEM((3, 3, part, padded), BF16),
            pltpu.VMEM((total, width), F32),
            dma((3,)),
            dma((2, n_chip)),
            dma((2, n_chip)),
            dma((2, n_chip)),
            dma((2, n_chip)),
            dma((3, 3, groups)),
            dma((3, 3, groups)),
            dma((3, groups)),
            dma((3, groups)),
        ],
        compiler_params=pltpu.CompilerParams(
            collective_id=0, has_side_effects=True, vmem_limit_bytes=67000000
        ),
    )(tokens, out_grad, gate_weight, up_weight, down_weight)

    inbound = [
        lax.ppermute(pieces[s], "col", [(i, (i + s) % n_col) for i in range(n_col)])
        for s in range(1, n_col)
    ]

    steps = 8
    rows = width // steps
    down_rows = -(-units // (steps * 128)) * 128
    gate_wgrad, up_wgrad, down_wgrad = pl.pallas_call(
        functools.partial(weight_kernel, units, 1.0 / math.sqrt(total)),
        grid=(steps,),
        out_shape=(
            jax.ShapeDtypeStruct((width, units), BF16),
            jax.ShapeDtypeStruct((width, units), BF16),
            jax.ShapeDtypeStruct((units, width), BF16),
        ),
        in_specs=[
            pl.BlockSpec((1, total, rows), lambda i: (0, 0, i)),
            pl.BlockSpec((1, total, width), lambda i: (1, 0, 0)),
            pl.BlockSpec((1, total, down_rows), lambda i: (0, 0, i)),
            pl.BlockSpec((1, total, padded), lambda i: (1, 0, 0)),
            pl.BlockSpec((1, total, padded), lambda i: (2, 0, 0)),
        ],
        out_specs=(
            pl.BlockSpec((rows, units), lambda i: (i, 0)),
            pl.BlockSpec((rows, units), lambda i: (i, 0)),
            pl.BlockSpec((down_rows, width), lambda i: (i, 0)),
        ),
        compiler_params=pltpu.CompilerParams(vmem_limit_bytes=48000000),
        cost_estimate=pl.CostEstimate(
            flops=6 * total * width * units,
            bytes_accessed=6 * width * units,
            transcendentals=0,
        ),
    )(pan, pan, res, res, res)

    input_grad = pieces[0].astype(F32)
    for block in inbound:
        input_grad = input_grad + block.astype(F32)
    return (input_grad.astype(BF16), gate_wgrad, up_wgrad, down_wgrad)


def solution(mesh):
    placed = (P("col", "row"), P("col", "row"), P("row", "col"), P("row", "col"), P("col", "row"))
    return jax.shard_map(
        functools.partial(local, mesh.shape["col"]),
        mesh=mesh,
        in_specs=placed,
        out_specs=(P("col", "row"), P("row", "col"), P("row", "col"), P("col", "row")),
        check_vma=False,
    )
```
